32 devices in a mesh: wide: 16 (over z, y, core), narrow: 2 (over x).
Axes of the slice: x: 2, y: 2, z: 4, core: 2. Of those that a mesh axis runs over, the one named last changes fastest.
Arguments:
- inputs: bfloat16 [2, 32, 128, 1024], P(None, ('wide', 'narrow')), may hold values from -6 to 6
- out_grad: bfloat16 [2, 32, 128, 1024], P(None, ('wide', 'narrow')), may hold values from -6 to 6
- group_id: int32 [2, 32], P(None, ('wide', 'narrow')), may hold values from 0 to 15
- group_count: int32 [16], replicated, may hold values from 1 to 4
- norm_gain: bfloat16 [4, 1024], P(None, 'narrow'), may hold values from 0.5 to 1.5
- norm_bias: bfloat16 [4, 1024], P(None, 'narrow'), may hold values from -1.25 to 1.25
- w_qkv: bfloat16 [1024, 3072], P('narrow'), may hold values from -0.1875 to 0.1875
- w_out: bfloat16 [1024, 1024], P('narrow'), may hold values from -1.5 to 1.5
- w_up: bfloat16 [1024, 4096], P('narrow'), may hold values from -0.1875 to 0.1875
- w_down: bfloat16 [4096, 1024], P('narrow'), may hold values from -0.09375 to 0.09375
- bias_model: bfloat16 [4, 1024], P(None, 'narrow'), may hold values from -0.625 to 0.625
- bias_up: bfloat16 [4096], P('narrow'), may hold values from -0.625 to 0.625
Outputs:
- output: bfloat16 [2, 32, 128, 1024], P(None, ('wide', 'narrow'))
- grad_input: bfloat16 [2, 32, 128, 1024], P(None, ('wide', 'narrow'))
- grad_norm_gain: float32 [4, 1024], P(None, 'narrow')
- grad_norm_bias: float32 [4, 1024], P(None, 'narrow')
- grad_qkv: float32 [1024, 3072], P('narrow')
- grad_out: float32 [1024, 1024], P('narrow')
- grad_up: float32 [1024, 4096], P('narrow')
- grad_down: float32 [4096, 1024], P('narrow')
- grad_bias_model: float32 [4, 1024], P(None, 'narrow')
- grad_bias_up: float32 [4096], P('narrow')
The draws below stay inside these ranges and needn't reach their ends.
All inputs are finite; a program needn't handle non-finite values.
Results may differ from the reference program's by a relative error of at most 0.02.
Values may be sent and summed in bfloat16 or wider, within the bound.
No kernel may reach another device: no remote copies, remote signals or barrier semaphores. Data moves between devices by JAX's collectives and lax.ppermute only.
A program may use at most 256 MiB of HBM per device.

```python
import math
import jax
import jax.numpy as jnp
from jax import lax

D = 1024
HEADS = 16
HEAD = 64
FF = 4096
MICRO = 2
GROUPS = 16
LEN = 128
BATCH = 32


def with_ends(drawn, rng, least, top_value):
    longest = drawn.shape.index(max(drawn.shape))
    spots = []
    for shift in (0, 1):
        where = [jax.random.randint(jax.random.fold_in(rng, axis), (), 0, length) for axis, length in enumerate(drawn.shape)]
        where[longest] = (where[longest] + shift) % drawn.shape[longest]
        spots.append(tuple(where))
    return drawn.at[spots[0]].set(least).at[spots[1]].set(top_value)


def levels(own_key, extent, shards, low, high):
    loudness, own = 1.0, jax.random.fold_in(own_key, 6)
    for dim, shards_of in shards:
        heights = jnp.exp(jax.random.uniform(jax.random.fold_in(own, dim), (shards_of,), jnp.float32, low / len(shards), high / len(shards)))
        loudness = loudness * jnp.repeat(heights, extent[dim] // shards_of).reshape([-1 if axis == dim else 1 for axis in range(len(extent))])
    return loudness


def noise(key, extent, scale, limit, cuts=(), kind=jnp.bfloat16):
    drawn = jax.random.normal(key, extent, jnp.float32) * scale
    if len(cuts) > 0:
        drawn = levels(key, extent, cuts, -0.22, 0.18) * drawn
    return jnp.clip(drawn, min=-limit, max=limit).astype(kind)


def setup_inputs(seed: int = 0) -> dict:
    arg_keys = jax.random.split(jax.random.key(seed), 13)
    return {
        "inputs": noise(arg_keys[0], (MICRO, BATCH, LEN, D), 1.0, 6.0, ((1, 32),)),
        "out_grad": noise(arg_keys[1], (MICRO, BATCH, LEN, D), 1.0, 6.0, ((1, 32),)),
        "group_id": with_ends(jax.random.randint(arg_keys[2], (MICRO, BATCH), 0, GROUPS), jax.random.fold_in(arg_keys[2], 1), 0, GROUPS - 1).astype(jnp.int32),
        "group_count": with_ends(jax.random.randint(arg_keys[3], (GROUPS,), 1, 5), jax.random.fold_in(arg_keys[3], 1), 1, 4).astype(jnp.int32),
        "norm_gain": jnp.clip(1.0 + 0.1 * jax.random.normal(arg_keys[4], (4, D), jnp.float32), 0.5, 1.5).astype(jnp.bfloat16),
        "norm_bias": noise(arg_keys[5], (4, D), 0.2, 1.25, ((1, 2),)),
        "w_qkv": noise(arg_keys[6], (D, 3 * D), D ** -0.5, 0.1875, ((0, 2),)),
        "w_out": noise(arg_keys[7], (D, D), (D // 64) ** -0.5, 1.5, ((0, 2),)),
        "w_up": noise(arg_keys[8], (D, FF), D ** -0.5, 0.1875, ((0, 2),)),
        "w_down": noise(arg_keys[9], (FF, D), FF ** -0.5, 0.09375, ((0, 2),)),
        "bias_model": noise(arg_keys[10], (4, D), 0.1, 0.625, ((1, 2),)),
        "bias_up": noise(arg_keys[11], (FF,), 0.1, 0.625, ((0, 2),)),
    }


@jax.custom_vjp
def low(v):
    return lax.optimization_barrier(v.astype(jnp.bfloat16)).astype(jnp.float32)

@jax.custom_vjp
def low_back(v):
    return v

def low_keep(v):
    return (low(v), None)

def low_pass(kept, grad):
    return (grad,)

def back_keep(v):
    return (v, None)

def back_low(kept, grad):
    return (low(grad),)
low.defvjp(low_keep, low_pass)
low_back.defvjp(back_keep, back_low)
HIGHEST = lax.Precision.HIGHEST
EPSILON = 1e-05
RELAX = 32.0

def layer_norm(value, gain, shift):
    average = lax.optimization_barrier(jnp.mean(value, axis=-1, keepdims=True))
    centred = value - average
    spread = lax.optimization_barrier(jnp.mean(centred * centred, axis=-1, keepdims=True))
    return centred * lax.rsqrt(spread + EPSILON) * gain + shift

def project(left, right):
    return jnp.einsum('nld,de->nle', left, right, precision=HIGHEST, preferred_element_type=jnp.float32)

def attend(qkv):
    length = qkv.shape[0]
    query = qkv[:, :D].reshape(length, HEADS, HEAD).transpose(1, 0, 2)
    keys = qkv[:, D:2 * D].reshape(length, HEADS, HEAD).transpose(1, 0, 2)
    values = qkv[:, 2 * D:].reshape(length, HEADS, HEAD).transpose(1, 0, 2)
    scores = jnp.einsum('hqd,hkd->hqk', query, keys, precision=HIGHEST) / (RELAX * math.sqrt(HEAD))
    rows = lax.broadcasted_iota(jnp.int32, (length, length), 0)
    columns = lax.broadcasted_iota(jnp.int32, (length, length), 1)
    scores = jnp.where(columns <= rows, scores, -1000000000.0)
    scores = low_back(scores)
    top = lax.optimization_barrier(jnp.max(scores, axis=-1, keepdims=True))
    probs = jax.nn.softmax(RELAX * (scores - top), axis=-1)
    weights = low(probs)
    mixed = jnp.einsum('hqk,hkd->hqd', weights, values, precision=HIGHEST)
    return mixed.transpose(1, 0, 2).reshape(length, D)

def layer(block, params):
    norm_gain, norm_bias, w_qkv, w_out, w_up, w_down, bias_model, bias_up = params
    first = low(layer_norm(block, norm_gain[0], norm_bias[0]))
    qkv_bias = jnp.concatenate([bias_model[0], jnp.zeros_like(bias_model[0]), bias_model[1]])
    qkv = low(low_back(project(first, w_qkv) + qkv_bias))
    mixed = lax.map(jax.checkpoint(attend), qkv)
    mixed = low(low_back(mixed))
    branch = low_back(project(mixed, w_out) + bias_model[2])
    middle = block + layer_norm(branch, norm_gain[1], norm_bias[1])
    third = low(layer_norm(middle, norm_gain[2], norm_bias[2]))
    hidden = low_back(project(third, w_up) + bias_up)
    active = low(jax.nn.gelu(hidden, approximate=False))
    second = low_back(project(active, w_down) + bias_model[3])
    return middle + layer_norm(second, norm_gain[3], norm_bias[3])

def reference(inputs, out_grad, group_id, group_count, norm_gain, norm_bias, w_qkv, w_out, w_up, w_down, bias_model, bias_up):
    params = tuple((p.astype(jnp.float32) for p in (norm_gain, norm_bias, w_qkv, w_out, w_up, w_down, bias_model, bias_up)))
    matches = group_id[:, :, None] == jnp.arange(GROUPS, dtype=jnp.int32)[None, None, :]
    counts = lax.optimization_barrier(jnp.sum(jnp.where(matches, group_count[None, None, :], 0), axis=-1))
    seq_scale = 1.0 / counts.astype(jnp.float32)
    total_seqs = MICRO * BATCH
    group_size = math.gcd(total_seqs, 8)
    blocks = total_seqs // group_size
    seqs = inputs.astype(jnp.float32).reshape(blocks, group_size, LEN, D)
    cots = (out_grad.astype(jnp.float32) * seq_scale[:, :, None, None]).reshape(blocks, group_size, LEN, D)

    def step(total, pieces):
        block, cot = pieces
        result, pull = jax.vjp(layer, block, params)
        grad_block, grad_params = pull(cot)
        total = jax.tree.map(lambda left, right: left + right, total, grad_params)
        return (total, (result.astype(jnp.bfloat16), grad_block.astype(jnp.bfloat16)))
    start = jax.tree.map(jnp.zeros_like, params)
    totals, (results, grads) = lax.scan(step, start, (seqs, cots))
    output = results.reshape(MICRO, BATCH, LEN, D)
    grad_input = grads.reshape(MICRO, BATCH, LEN, D)
    return (output, grad_input, totals[0], totals[1], totals[2], totals[3], totals[4], totals[5], totals[6], totals[7])
```

```python
import math

import jax
import jax.numpy as jnp
from jax import lax
from jax.sharding import PartitionSpec as P

HEADS = 16
EPSILON = 1e-05
RELAX = 32.0


def layer_norm(value, gain, shift):
    average = jnp.mean(value, axis=-1, keepdims=True)
    centred = value - average
    spread = jnp.mean(centred * centred, axis=-1, keepdims=True)
    return centred * lax.rsqrt(spread + EPSILON) * gain + shift


def exact_gelu(value):
    return jax.nn.gelu(value, approximate=False)


def weight_grad(left, grad):
    return lax.dot_general(left, grad, (((0,), (0,)), ((), ())), preferred_element_type=jnp.float32)


def column_sum(grad):
    return jnp.sum(grad.astype(jnp.float32), axis=0)


def rows_of(value, start, count):
    return lax.dynamic_slice_in_dim(value, start, count, axis=0)


def columns_of(value, start, count):
    return lax.dynamic_slice_in_dim(value, start, count, axis=1)


class Place:
    def __init__(self):
        self.n = lax.axis_size("narrow")
        self.w = lax.axis_size("wide")
        self.x = lax.axis_index("narrow")
        self.at = lax.axis_index("wide")
        self.masks = [1 << k for k in range(self.w.bit_length() - 1)]
        assert self.w == 1 << len(self.masks) and len(self.masks) >= 3

    def bit(self, mask):
        return (self.at // mask) % 2

    def flip(self, value, mask):
        return lax.ppermute(value, "wide", [(i, i ^ mask) for i in range(self.w)])

    def fetch(self, value, step):
        return lax.ppermute(value, "narrow", [(i, (i - step) % self.n) for i in range(self.n)])

    def give(self, value, step):
        return lax.ppermute(value, "narrow", [(i, (i + step) % self.n) for i in range(self.n)])

    def shard(self, step):
        return (self.x + step) % self.n

    def join(self, own, other, mask):
        return jnp.where(
            self.bit(mask) == 0,
            jnp.concatenate([own, other], axis=0),
            jnp.concatenate([other, own], axis=0),
        )


def gather_parts(place, shard, first, second):
    rows = shard.shape[0]
    half, piece = rows // 2, rows // 8
    core = place.bit(1)
    start = core * half + place.bit(second) * (2 * piece) + place.bit(first) * piece
    own = rows_of(shard, start, piece)
    parts = [(place.x * rows, shard)]
    for step in range(1, place.n):
        got = place.fetch(own, step)
        got = place.join(got, place.flip(got, first), first)
        got = place.join(got, place.flip(got, second), second)
        base = place.shard(step) * rows
        parts.append((base + core * half, got))
        parts.append((base + (1 - core) * half, place.flip(got, 1)))
    return parts


def forward_product(left, parts):
    total = None
    for start, rows in parts:
        term = jnp.dot(columns_of(left, start, rows.shape[0]), rows, preferred_element_type=jnp.float32)
        total = term if total is None else total + term
    return total


def back_product(grad, parts, width):
    out = jnp.zeros((grad.shape[0], width), jnp.float32)
    for start, rows in parts:
        term = lax.dot_general(grad, rows, (((1,), (1,)), ((), ())), preferred_element_type=jnp.float32)
        out = lax.dynamic_update_slice_in_dim(out, term, start, axis=1)
    return out


def add_low(left, right):
    return (left.astype(jnp.float32) + right.astype(jnp.float32)).astype(jnp.bfloat16)


def reduce_grad(place, left, grad):
    rows = left.shape[1] // place.n
    half = rows // 2
    core = place.bit(1)
    sums = {}
    for step in list(range(1, place.n)) + [0]:
        base = place.shard(step) * rows
        theirs = columns_of(left, base + (1 - core) * half, half)
        mine = columns_of(left, base + core * half, half)
        sent = place.flip(weight_grad(theirs, grad).astype(jnp.bfloat16), 1)
        sums[step] = (weight_grad(mine, grad) + sent.astype(jnp.float32)).astype(jnp.bfloat16)
    terms = [sums[0]] + [place.give(sums[step], step) for step in range(1, place.n)]
    size = half

    def total(pieces):
        value = pieces[0].astype(jnp.float32)
        for piece in pieces[1:]:
            value = value + piece.astype(jnp.float32)
        return value.astype(jnp.bfloat16)

    for mask in place.masks[1:]:
        size //= 2
        bit = place.bit(mask)
        sent = total([rows_of(term, (1 - bit) * size, size) for term in terms])
        kept = total([rows_of(term, bit * size, size) for term in terms])
        terms = [kept, place.flip(sent, mask)]
    value = total(terms)
    for mask in reversed(place.masks[1:]):
        value = place.join(value, place.flip(value, mask), mask)
    return place.join(value, place.flip(value, 1), 1).astype(jnp.float32)


def reduce_columns(place, left, grad, chunks):
    width = grad.shape[1] // chunks
    return jnp.concatenate(
        [reduce_grad(place, left, grad[:, k * width : (k + 1) * width]) for k in range(chunks)], axis=1
    )


def split_heads(qkv, seqs, heads):
    length = qkv.shape[0] // seqs
    width = qkv.shape[1] // 3
    parts = qkv.reshape(seqs, length, 3, heads, width // heads)
    return (parts[:, :, 0], parts[:, :, 1], parts[:, :, 2])


def raw_scores(query, keys):
    length = query.shape[1]
    scale = RELAX * math.sqrt(query.shape[-1])
    scores = jnp.einsum("sqhd,skhd->shqk", query, keys, preferred_element_type=jnp.float32) / scale
    rows = lax.broadcasted_iota(jnp.int32, (length, length), 0)
    columns = lax.broadcasted_iota(jnp.int32, (length, length), 1)
    return jnp.where(columns <= rows, scores, -1000000000.0)


def attention(qkv, seqs, heads):
    query, keys, values = split_heads(qkv, seqs, heads)
    scores = raw_scores(query, keys)
    top = jnp.max(scores, axis=-1, keepdims=True)
    exps = jnp.exp(RELAX * (scores - top))
    probs = exps / jnp.sum(exps, axis=-1, keepdims=True)
    weights = probs.astype(jnp.bfloat16)
    mixed = jnp.einsum("shqk,skhd->sqhd", weights, values, preferred_element_type=jnp.float32)
    return mixed.reshape(qkv.shape[0], qkv.shape[1] // 3).astype(jnp.bfloat16), probs


def attention_back(qkv, probs, grad_mixed, seqs, heads):
    query, keys, values = split_heads(qkv, seqs, heads)
    weights = probs.astype(jnp.bfloat16)
    tokens, width = grad_mixed.shape
    grad_heads = grad_mixed.reshape(seqs, tokens // seqs, heads, width // heads)
    grad_weights = jnp.einsum("sqhd,skhd->shqk", grad_heads, values, preferred_element_type=jnp.float32)
    inner = jnp.sum(probs * grad_weights, axis=-1, keepdims=True)
    grad_scores = (RELAX * probs * (grad_weights - inner)).astype(jnp.bfloat16)
    scale = RELAX * math.sqrt(query.shape[-1])
    grad_query = jnp.einsum("shqk,skhd->sqhd", grad_scores, keys, preferred_element_type=jnp.float32) / scale
    grad_keys = jnp.einsum("shqk,sqhd->skhd", grad_scores, query, preferred_element_type=jnp.float32) / scale
    grad_values = jnp.einsum("shqk,sqhd->skhd", weights, grad_heads, preferred_element_type=jnp.float32)
    stacked = jnp.stack([grad_query, grad_keys, grad_values], axis=2)
    return stacked.reshape(tokens, 3 * width).astype(jnp.bfloat16)


def gather_small(place, norm_gain, norm_bias, bias_model, bias_up):
    part = norm_gain.shape[1]
    packed = jnp.concatenate([norm_gain, norm_bias, bias_model, bias_up.reshape(-1, part)], axis=0)
    pieces = [packed] + [place.fetch(packed, step) for step in range(1, place.n)]
    stacked = jnp.roll(jnp.stack(pieces), place.x, axis=0).astype(jnp.float32)
    width = part * place.n
    rows = stacked.transpose(1, 0, 2)[:12].reshape(12, width)
    return rows[0:4], rows[4:8], rows[8:12], stacked[:, 12:].reshape(bias_up.shape[0] * place.n)


def reduce_small(place, gain, shift, bias, hidden):
    part = gain.shape[1] // place.n
    rows = jnp.concatenate([gain, shift, bias], axis=0).reshape(12, place.n, part).transpose(1, 0, 2)
    packed = jnp.concatenate([rows, hidden.reshape(place.n, -1, part)], axis=1)

    def block(step):
        return lax.dynamic_index_in_dim(packed, place.shard(step), axis=0, keepdims=False)

    value = block(0)
    for step in range(1, place.n):
        value = value + place.give(block(step), step)
    for mask in place.masks:
        value = value + place.flip(value, mask)
    return value[0:4], value[4:8], value[8:12], value[12:].reshape(-1)


def on_device(
    inputs,
    out_grad,
    group_id,
    group_count,
    norm_gain,
    norm_bias,
    w_qkv,
    w_out,
    w_up,
    w_down,
    bias_model,
    bias_up,
):
    place = Place()
    micros, held, length, width = inputs.shape
    seqs = micros * held
    tokens = seqs * length
    matches = group_id[:, :, None] == jnp.arange(group_count.shape[0], dtype=jnp.int32)[None, None, :]
    counts = jnp.sum(jnp.where(matches, group_count[None, None, :], 0), axis=-1)
    seq_scale = 1.0 / counts.astype(jnp.float32)
    gain, shift, bias, bias_hidden = gather_small(place, norm_gain, norm_bias, bias_model, bias_up)
    y, z = place.masks[1], place.masks[2]
    qkv_parts = gather_parts(place, w_qkv, y, z)
    out_parts = gather_parts(place, w_out, z, y)
    up_parts = gather_parts(place, w_up, z, y)
    down_parts = gather_parts(place, w_down, y, z)

    block = inputs.reshape(tokens, width).astype(jnp.float32)
    qkv_bias = jnp.concatenate([bias[0], jnp.zeros((width,), jnp.float32), bias[1]])
    first = layer_norm(block, gain[0], shift[0]).astype(jnp.bfloat16)
    qkv = (forward_product(first, qkv_parts) + qkv_bias).astype(jnp.bfloat16)
    mixed, probs = attention(qkv, seqs, HEADS)
    branch = forward_product(mixed, out_parts) + bias[2]
    middle = block + layer_norm(branch, gain[1], shift[1])
    third = layer_norm(middle, gain[2], shift[2]).astype(jnp.bfloat16)
    hidden = forward_product(third, up_parts) + bias_hidden
    active = exact_gelu(hidden).astype(jnp.bfloat16)
    second = forward_product(active, down_parts) + bias[3]
    result = (middle + layer_norm(second, gain[3], shift[3])).astype(jnp.bfloat16)

    cotangent = out_grad.astype(jnp.float32) * seq_scale[:, :, None, None]
    cotangent = cotangent.reshape(tokens, width)
    unused_last, pull_last = jax.vjp(layer_norm, second, gain[3], shift[3])
    grad_second, gain_last, shift_last = pull_last(cotangent)
    grad_second = grad_second.astype(jnp.bfloat16)
    grad_down = reduce_columns(place, active, grad_second, 2)
    bias_down = column_sum(grad_second)
    grad_active = back_product(grad_second, down_parts, active.shape[1])
    unused_gelu, pull_gelu = jax.vjp(exact_gelu, hidden)
    grad_hidden = pull_gelu(grad_active)[0].astype(jnp.bfloat16)
    grad_up = reduce_columns(place, third, grad_hidden, 2)
    bias_up_sum = column_sum(grad_hidden)
    grad_third = back_product(grad_hidden, up_parts, width)
    unused_third, pull_third = jax.vjp(layer_norm, middle, gain[2], shift[2])
    grad_inner, gain_third, shift_third = pull_third(grad_third)
    grad_middle = cotangent + grad_inner
    unused_branch, pull_branch = jax.vjp(layer_norm, branch, gain[1], shift[1])
    grad_branch, gain_branch, shift_branch = pull_branch(grad_middle)
    grad_branch = grad_branch.astype(jnp.bfloat16)
    grad_out = reduce_columns(place, mixed, grad_branch, 1)
    bias_out = column_sum(grad_branch)
    grad_mixed = back_product(grad_branch, out_parts, width).astype(jnp.bfloat16)
    grad_qkv = attention_back(qkv, probs, grad_mixed, seqs, HEADS)
    grad_project = reduce_columns(place, first, grad_qkv, 2)
    qkv_sums = column_sum(grad_qkv)
    grad_first = back_product(grad_qkv, qkv_parts, width)
    unused_first, pull_first = jax.vjp(layer_norm, block, gain[0], shift[0])
    grad_block, gain_first, shift_first = pull_first(grad_first)
    grad_input = (grad_middle + grad_block).astype(jnp.bfloat16)
    small = reduce_small(
        place,
        jnp.stack([gain_first, gain_branch, gain_third, gain_last]),
        jnp.stack([shift_first, shift_branch, shift_third, shift_last]),
        jnp.stack([qkv_sums[:width], qkv_sums[2 * width :], bias_out, bias_down]),
        bias_up_sum,
    )
    return (
        result.reshape(inputs.shape),
        grad_input.reshape(inputs.shape),
        small[0],
        small[1],
        grad_project,
        grad_out,
        grad_up,
        grad_down,
        small[2],
        small[3],
    )


def solution(mesh):
    tokens = P(None, ("wide", "narrow"), None, None)
    groups = P(None, ("wide", "narrow"))
    columns, rows, line = P(None, "narrow"), P("narrow", None), P("narrow")
    params = (columns, columns, rows, rows, rows, rows, columns, line)
    return jax.shard_map(
        on_device,
        mesh=mesh,
        in_specs=(tokens, tokens, groups, P()) + params,
        out_specs=(tokens, tokens) + params,
        check_vma=False,
    )
```
